32 devices in a mesh: tm: 4 (over x, core), space: 8 (over z, y).
Axes of the slice: x: 2, y: 2, z: 4, core: 2. Of those that a mesh axis runs over, the one named last changes fastest.
Arguments:
- frames_in: bfloat16 [24, 64, 128, 128], P('tm', 'space'), may hold values from -6 to 6
- boundary: bfloat16 [5, 2, 128, 128], replicated, may hold values from -6 to 6
- conv_first: bfloat16 [3, 3, 128, 128], replicated, may hold values from -0.1875 to 0.1875
- conv_second: bfloat16 [3, 3, 128, 128], replicated, may hold values from -0.1875 to 0.1875
- norm_gain: float32 [128], replicated, may hold values from 0.1 to 1.9
- qkv_weight: bfloat16 [128, 384], replicated, as said below
- out_weight: bfloat16 [128, 128], replicated, may hold values from -0.5 to 0.5
Outputs:
- block_out: bfloat16 [24, 64, 128, 128], P('tm', 'space')
The draws below stay inside these ranges and needn't reach their ends.
Inputs may be any that keep to these rules, and one draw needn't show every extreme that they name: `qkv_weight`: a projection matrix.
All inputs are finite; a program needn't handle non-finite values.
Results may differ from the reference program's by a relative error of at most 0.034.
The reference program's roundings to bfloat16 on the way count: a program that leaves them out, or rounds other values in their place, can miss the bound.
Values may be sent and summed in bfloat16 or wider, within the bound.
A program may use at most 128 MiB of HBM per device.

```python
import math
import jax
import jax.numpy as jnp
from jax import lax

CH = 128
HEADS = 8
FRAMES = 24
COARSE = 5
COLS = 128
ROWS = 64


def draw_qkv_weight(key, part):
    base = jax.random.normal(key, (CH, 3 * CH), jnp.float32)
    factor = 1.0
    return (jnp.clip(base, -4.0, 4.0) * (factor / math.sqrt(CH))).astype(jnp.bfloat16)


def block_levels(own_key, extent, cuts, least, largest):
    def one(position, blocks):
        draws = jax.random.uniform(jax.random.fold_in(jax.random.fold_in(own_key, 6), position), (blocks,), jnp.float32, least / len(cuts), largest / len(cuts))
        return jnp.repeat(jnp.exp(draws), extent[position] // blocks).reshape((-1,) + (1,) * (len(extent) - position - 1))

    factor_of = one(*cuts[0])
    for cut in cuts[1:]:
        factor_of = factor_of * one(*cut)
    return factor_of


def normal_values(own_key, shape, scale, bound, cuts=(), kind=jnp.bfloat16):
    level = block_levels(own_key, shape, cuts, -0.22, 0.18) if cuts else 1.0
    result = jax.random.normal(own_key, shape, jnp.float32) * scale * level
    return jnp.minimum(jnp.maximum(result, -bound), bound).astype(kind)


def setup_inputs(seed: int = 0) -> dict:
    streams_of = jax.random.split(jax.random.key(seed), 8)
    frames_in = normal_values(streams_of[0], (FRAMES, ROWS, COLS, CH), 1.0, 6.0, ((0, 4), (1, 8)))
    boundary = normal_values(streams_of[1], (COARSE, 2, COLS, CH), 1.0, 6.0)
    conv_first = normal_values(streams_of[2], (3, 3, CH, CH), (9 * CH) ** -0.5, 0.1875)
    conv_second = normal_values(streams_of[3], (3, 3, CH, CH), (9 * CH) ** -0.5, 0.1875)
    norm_gain = jnp.clip(1.0 + 0.18 * jax.random.normal(streams_of[4], (CH,), jnp.float32), 0.1, 1.9)
    qkv_weight = draw_qkv_weight(jax.random.fold_in(streams_of[7], 71), 0)
    out_weight = normal_values(streams_of[6], (CH, CH), CH ** -0.5, 0.5)
    return {"frames_in": frames_in, "boundary": boundary, "conv_first": conv_first, "conv_second": conv_second, "norm_gain": norm_gain, "qkv_weight": qkv_weight, "out_weight": out_weight}


def interp_matrix(times):
    scaled = times * (COARSE - 1)
    lower = scaled // (FRAMES - 1)
    upper = jnp.minimum(lower + 1, COARSE - 1)
    frac = (scaled - lower * (FRAMES - 1)).astype(jnp.float32) / float(FRAMES - 1)
    levels = jnp.arange(COARSE, dtype=jnp.int32)
    low_hot = (levels[None, :] == lower[:, None]).astype(jnp.float32)
    up_hot = (levels[None, :] == upper[:, None]).astype(jnp.float32)
    return (1.0 - frac)[:, None] * low_hot + frac[:, None] * up_hot

def conv_frame(padded, kernel):
    rows = padded.shape[0] - 2
    width = padded.shape[1] - 2
    chans = padded.shape[2]
    total = jnp.zeros((rows * width, kernel.shape[3]), jnp.float32)
    for shift_r in range(3):
        for shift_c in range(3):
            piece = padded[shift_r:shift_r + rows, shift_c:shift_c + width].reshape(rows * width, chans)
            total = total + jnp.dot(piece, kernel[shift_r, shift_c], preferred_element_type=jnp.float32)
    return total.reshape(rows, width, kernel.shape[3])

def extend_frame(frame, strip):
    rows = jnp.concatenate([strip[0:1], frame, strip[1:2]], axis=0)
    return jnp.pad(rows, ((0, 0), (1, 1), (0, 0)))

def temporal(resid, norm_gain, qkv_weight, out_weight):
    nframes, pixels, chans = resid.shape
    head_dim = chans // HEADS
    rf = resid.astype(jnp.float32)
    normed = (rf * lax.rsqrt(lax.optimization_barrier(jnp.mean(rf * rf, axis=-1, keepdims=True)) + 1e-06) * norm_gain).astype(jnp.bfloat16)
    qkv = jnp.dot(normed.reshape(nframes * pixels, chans), qkv_weight, preferred_element_type=jnp.float32)
    qkv = qkv.astype(jnp.bfloat16).reshape(nframes, pixels, 3, HEADS, head_dim)
    query = qkv[:, :, 0].astype(jnp.float32)
    key_part = qkv[:, :, 1].astype(jnp.float32)
    value = qkv[:, :, 2].astype(jnp.float32)
    scores = jnp.einsum('fphd,gphd->phfg', query, key_part) * (1.0 / head_dim ** 0.5)
    top = lax.optimization_barrier(jnp.max(scores, axis=-1, keepdims=True))
    expd = jnp.exp(scores - top)
    probs = (expd / lax.optimization_barrier(jnp.sum(expd, axis=-1, keepdims=True))).astype(jnp.bfloat16)
    attended = jnp.einsum('phfg,gphd->fphd', probs.astype(jnp.float32), value).astype(jnp.bfloat16)
    proj = jnp.dot(attended.reshape(nframes * pixels, chans), out_weight, preferred_element_type=jnp.float32)
    return (rf.reshape(nframes * pixels, chans) + proj).astype(jnp.bfloat16).reshape(nframes, pixels, chans)

def reference(frames_in, boundary, conv_first, conv_second, norm_gain, qkv_weight, out_weight):
    times = jnp.arange(FRAMES, dtype=jnp.int32)
    weights = interp_matrix(times)
    strips = jnp.einsum('tk,kscx->tscx', weights, boundary.astype(jnp.float32)).astype(jnp.bfloat16)

    def one_frame(pair):
        frame, strip = pair
        first = conv_frame(extend_frame(frame, strip), conv_first)
        hidden = jax.nn.silu(first).astype(jnp.bfloat16)
        second = conv_frame(extend_frame(hidden, strip), conv_second)
        return (frame.astype(jnp.float32) + second).astype(jnp.bfloat16)
    resid = lax.map(one_frame, (frames_in, strips))
    by_rows = jnp.swapaxes(resid, 0, 1)

    def one_row(row_block):
        return temporal(row_block, norm_gain, qkv_weight, out_weight)
    mixed = lax.map(one_row, by_rows)
    return jnp.swapaxes(mixed, 0, 1)
```

```python
import jax
import jax.numpy as jnp
from jax import lax
from jax.experimental import pallas as pl
from jax.experimental.pallas import tpu as pltpu
from jax.sharding import PartitionSpec as P

HEADS = 8
FRAMES = 24
COARSE = 5


def padded_2(cells, sides, width):
    for axis, dim in sides:
        count = lax.axis_size(axis)
        ends = count - 1
        head = lax.slice_in_dim(cells, 0, width, axis=dim)
        tail = lax.slice_in_dim(cells, cells.shape[dim] - width, cells.shape[dim], axis=dim)
        cells = jnp.concatenate(
            [
                lax.ppermute(tail, axis, [(i, (i + 1) % count) for i in range(ends)]),
                cells,
                lax.ppermute(head, axis, [((i + 1) % count, i) for i in range(ends)]),
            ],
            axis=dim,
        )
    return cells


def interp_matrix(times):
    scaled = times * (COARSE - 1)
    lower = scaled // (FRAMES - 1)
    upper = jnp.minimum(lower + 1, COARSE - 1)
    frac = (scaled - lower * (FRAMES - 1)).astype(jnp.float32) / float(FRAMES - 1)
    levels = jnp.arange(COARSE, dtype=jnp.int32)
    low_hot = (levels[None, :] == lower[:, None]).astype(jnp.float32)
    up_hot = (levels[None, :] == upper[:, None]).astype(jnp.float32)
    return (1.0 - frac)[:, None] * low_hot + frac[:, None] * up_hot


def fix_edges(padded, strips):
    place = lax.axis_index("space")
    last = lax.axis_size("space") - 1
    top_row = jnp.where(place == 0, strips[:, 0:1], padded[:, 0:1])
    bottom_row = jnp.where(place == last, strips[:, 1:2], padded[:, -1:])
    rows = jnp.concatenate([top_row, padded[:, 1:-1], bottom_row], axis=1)
    return jnp.pad(rows, ((0, 0), (0, 0), (1, 1), (0, 0)))


def conv_tile(padded, kernel):
    nframes = padded.shape[0]
    rows = padded.shape[1] - 2
    width = padded.shape[2] - 2
    chans = padded.shape[3]
    total = jnp.zeros((nframes * rows * width, kernel.shape[3]), jnp.float32)
    for shift_r in range(3):
        for shift_c in range(3):
            piece = padded[:, shift_r : shift_r + rows, shift_c : shift_c + width].reshape(
                nframes * rows * width, chans
            )
            total = total + jnp.dot(
                piece, kernel[shift_r, shift_c], preferred_element_type=jnp.float32
            )
    return total.reshape(nframes, rows, width, kernel.shape[3])


def attend_pixels(x, qkv_weight, norm_gain, out_weight, mask, heads_of):
    nframes, group, chans = x.shape
    rows = nframes * group
    head_dim = chans // HEADS
    x = x.reshape(rows, chans)
    mean_sq = jnp.mean(x * x, axis=-1, keepdims=True)
    normed = (x * lax.rsqrt(mean_sq + 1e-06) * norm_gain).astype(jnp.bfloat16)
    qkv = jnp.dot(normed, qkv_weight, preferred_element_type=jnp.float32).astype(jnp.bfloat16)
    query = qkv[:, :chans] * jnp.bfloat16(1.0 / head_dim**0.5)
    key_part = qkv[:, chans : 2 * chans]
    value = qkv[:, 2 * chans :]
    with_ones = jnp.concatenate([value, jnp.ones_like(value)], axis=1)
    num = jnp.zeros((rows, chans), jnp.float32)
    den = jnp.ones((rows, chans), jnp.float32)
    for head in range(HEADS):
        own = heads_of == head
        picked = jnp.where(own, query, jnp.zeros_like(query))
        scores = lax.dot_general(
            picked, key_part, (((1,), (1,)), ((), ())), preferred_element_type=jnp.float32
        )
        scores = scores + mask
        top = jnp.max(scores, axis=-1, keepdims=True)
        expd = jnp.exp(scores - top).astype(jnp.bfloat16)
        both = jnp.dot(expd, with_ones, preferred_element_type=jnp.float32)
        num = jnp.where(own, both[:, :chans], num)
        den = jnp.where(own, both[:, chans:], den)
    attended = (num / den).astype(jnp.bfloat16)
    out = x + jnp.dot(attended, out_weight, preferred_element_type=jnp.float32)
    return out.reshape(nframes, group, chans)


def temporal_kernel(x_ref, gain_ref, qkv_ref, outw_ref, o_ref, mask_ref):
    nframes, pixels, chans = x_ref.shape
    rows = nframes * 8
    row = lax.broadcasted_iota(jnp.int32, (rows, rows), 0)
    col = lax.broadcasted_iota(jnp.int32, (rows, rows), 1)
    mask_ref[...] = jnp.where(lax.rem(row, 8) == lax.rem(col, 8), 0.0, -1e30)
    heads_of = lax.broadcasted_iota(jnp.int32, (rows, chans), 1) // (chans // HEADS)

    def step(i, carry):
        start = pl.multiple_of(i * 16, 16)
        x = x_ref[:, pl.ds(start, 16), :].astype(jnp.float32)
        halves = [
            attend_pixels(
                x[:, k * 8 : k * 8 + 8], qkv_ref[...], gain_ref[...], outw_ref[...],
                mask_ref[...], heads_of,
            )
            for k in range(2)
        ]
        o_ref[:, pl.ds(start, 16), :] = jnp.concatenate(halves, axis=1).astype(o_ref.dtype)
        return carry

    lax.fori_loop(0, pixels // 16, step, 0)


def temporal(resid, norm_gain, qkv_weight, out_weight):
    nframes, pixels, chans = resid.shape
    vmem = pl.BlockSpec(memory_space=pltpu.VMEM)
    return pl.pallas_call(
        temporal_kernel,
        out_shape=jax.ShapeDtypeStruct(resid.shape, resid.dtype),
        in_specs=[vmem] * 4,
        out_specs=vmem,
        scratch_shapes=[pltpu.VMEM((nframes * 8, nframes * 8), jnp.float32)],
        name="temporal",
    )(resid, norm_gain.reshape(1, chans), qkv_weight, out_weight)


def on_device(frames_in, boundary, conv_first, conv_second, norm_gain, qkv_weight, out_weight):
    local_frames = frames_in.shape[0]
    chans = frames_in.shape[3]
    times = lax.axis_index("tm") * local_frames + jnp.arange(local_frames, dtype=jnp.int32)
    weights = interp_matrix(times)
    strips = jnp.einsum("tk,kscx->tscx", weights, boundary.astype(jnp.float32)).astype(jnp.bfloat16)
    padded_in = padded_2(frames_in, (("space", 1),), 1)
    first = conv_tile(fix_edges(padded_in, strips), conv_first)
    hidden = jax.nn.silu(first).astype(jnp.bfloat16)
    padded_hidden = padded_2(hidden, (("space", 1),), 1)
    second = conv_tile(fix_edges(padded_hidden, strips), conv_second)
    resid = (frames_in.astype(jnp.float32) + second).astype(jnp.bfloat16)
    regrouped = lax.all_to_all(resid, "tm", split_axis=1, concat_axis=0, tiled=True)
    layout = regrouped.shape
    mixed = temporal(regrouped.reshape(FRAMES, -1, chans), norm_gain, qkv_weight, out_weight)
    return lax.all_to_all(
        mixed.reshape(layout), "tm", split_axis=0, concat_axis=1, tiled=True
    )


def solution(mesh):
    placed = (P("tm", "space", None, None), P(), P(), P(), P(), P(), P())
    return jax.shard_map(
        on_device,
        mesh=mesh,
        in_specs=placed,
        out_specs=P("tm", "space", None, None),
        check_vma=False,
    )
```

```python
import functools

import jax
import jax.numpy as jnp
from jax import lax
from jax.experimental import pallas as pl
from jax.experimental.pallas import tpu as pltpu
from jax.sharding import PartitionSpec as P

HEADS = 8
FRAMES = 24
COARSE = 5


def interp_matrix(times):
    scaled = times * (COARSE - 1)
    lower = scaled // (FRAMES - 1)
    upper = jnp.minimum(lower + 1, COARSE - 1)
    frac = (scaled - lower * (FRAMES - 1)).astype(jnp.float32) / float(FRAMES - 1)
    levels = jnp.arange(COARSE, dtype=jnp.int32)
    low_hot = (levels[None, :] == lower[:, None]).astype(jnp.float32)
    up_hot = (levels[None, :] == upper[:, None]).astype(jnp.float32)
    return (1.0 - frac)[:, None] * low_hot + frac[:, None] * up_hot


def attend_pixels(x, qkv_weight, norm_gain, out_weight, mask, heads_of):
    nframes, group, chans = x.shape
    rows = nframes * group
    head_dim = chans // HEADS
    x = x.reshape(rows, chans)
    mean_sq = jnp.mean(x * x, axis=-1, keepdims=True)
    normed = (x * lax.rsqrt(mean_sq + 1e-06) * norm_gain).astype(jnp.bfloat16)
    qkv = jnp.dot(normed, qkv_weight, preferred_element_type=jnp.float32).astype(jnp.bfloat16)
    query = qkv[:, :chans] * jnp.bfloat16(1.0 / head_dim**0.5)
    key_part = qkv[:, chans : 2 * chans]
    value = qkv[:, 2 * chans :]
    with_ones = jnp.concatenate([value, jnp.ones_like(value)], axis=1)
    num = jnp.zeros((rows, chans), jnp.float32)
    den = jnp.ones((rows, chans), jnp.float32)
    for head in range(HEADS):
        own = heads_of == head
        picked = jnp.where(own, query, jnp.zeros_like(query))
        scores = lax.dot_general(
            picked, key_part, (((1,), (1,)), ((), ())), preferred_element_type=jnp.float32
        )
        scores = scores + mask
        top = jnp.max(scores, axis=-1, keepdims=True)
        expd = jnp.exp(scores - top).astype(jnp.bfloat16)
        both = jnp.dot(expd, with_ones, preferred_element_type=jnp.float32)
        num = jnp.where(own, both[:, :chans], num)
        den = jnp.where(own, both[:, chans:], den)
    attended = (num / den).astype(jnp.bfloat16)
    out = x + jnp.dot(attended, out_weight, preferred_element_type=jnp.float32)
    return out.reshape(nframes, group, chans)


MESH = pl.DeviceIdType.MESH
STEP = 16
CHUNK = 4


def conv_taps(taps, weight, width):
    cells = jnp.concatenate(taps, axis=1)
    rows = cells.shape[0]
    chans = weight.shape[1] // 3
    wide = jnp.dot(cells, weight, preferred_element_type=jnp.float32)
    col = lax.rem(lax.broadcasted_iota(jnp.int32, (rows, chans), 0), width)
    left = jnp.where(col == 0, 0.0, pltpu.roll(wide[:, :chans], 1, 0))
    right = jnp.where(col == width - 1, 0.0, pltpu.roll(wide[:, 2 * chans :], rows - 1, 0))
    return wide[:, chans : 2 * chans] + left + right


def block_kernel(
    peers, spaces,
    x_ref, strips_ref, w1_ref, w2_ref, gain_ref, qkv_ref, outw_ref, o_ref,
    xpad, hpad, sbuf, rbuf, abuf, wcat, mask_ref,
    local_sem, halo_send, halo_recv, there_send, there_recv, back_send, back_recv, own_sem,
):
    nloc, rows, width, chans = x_ref.shape
    nframes = nloc * peers
    share = rows // peers
    me = lax.axis_index("tm")
    place = lax.axis_index("space")
    last = spaces - 1

    def peer_of(k):
        chip = lax.rem(me // 2 + k // 2, peers // 2)
        return chip * 2 + lax.rem(me + k % 2, 2)

    own_rows = pltpu.make_async_copy(x_ref, xpad.at[:, pl.ds(2, rows)], local_sem)
    own_rows.start()

    barrier = pltpu.get_barrier_semaphore()
    for k in range(1, peers):
        pl.semaphore_signal(barrier, inc=1, device_id={"tm": peer_of(k)}, device_id_type=MESH)

    @pl.when(place > 0)
    def _():
        pl.semaphore_signal(barrier, inc=1, device_id={"space": place - 1}, device_id_type=MESH)

    @pl.when(place < last)
    def _():
        pl.semaphore_signal(barrier, inc=1, device_id={"space": place + 1}, device_id_type=MESH)

    beside = jnp.where(place > 0, 1, 0) + jnp.where(place < last, 1, 0)
    pl.semaphore_wait(barrier, peers - 1 + beside)

    up = pltpu.make_async_remote_copy(
        x_ref.at[:, pl.ds(0, 2)], xpad.at[:, pl.ds(rows + 2, 2)],
        halo_send.at[0], halo_recv.at[0], device_id={"space": place - 1}, device_id_type=MESH,
    )
    down = pltpu.make_async_remote_copy(
        x_ref.at[:, pl.ds(rows - 2, 2)], xpad.at[:, pl.ds(0, 2)],
        halo_send.at[1], halo_recv.at[1], device_id={"space": place + 1}, device_id_type=MESH,
    )

    @pl.when(place > 0)
    def _():
        up.start()

    @pl.when(place < last)
    def _():
        down.start()

    for which, ref in enumerate((w1_ref, w2_ref)):
        for dy in range(3):
            for dx in range(3):
                wcat[which, dy * chans : (dy + 1) * chans, dx * chans : (dx + 1) * chans] = ref[dy, dx]
    group = nframes * 8
    row_id = lax.broadcasted_iota(jnp.int32, (group, group), 0)
    col_id = lax.broadcasted_iota(jnp.int32, (group, group), 1)
    mask_ref[...] = jnp.where(lax.rem(row_id, 8) == lax.rem(col_id, 8), 0.0, -1e30)
    heads_of = lax.broadcasted_iota(jnp.int32, (group, chans), 1) // (chans // HEADS)

    def hidden_rows(frame, row):
        taps = [xpad[frame, row + dy : row + dy + 2].reshape(2 * width, chans) for dy in range(3)]
        first = conv_taps(taps, wcat[0], width)
        act = (first / (1.0 + jnp.exp(-first))).astype(jnp.bfloat16)
        hpad[frame, row : row + 2] = act.reshape(2, width, chans)

    own_rows.wait()

    def interior(frame, carry):
        for row in range(2, rows, 2):
            hidden_rows(frame, row)
        return carry

    lax.fori_loop(0, nloc, interior, 0)

    @pl.when(place > 0)
    def _():
        down.wait_recv()

    @pl.when(place == 0)
    def _():
        xpad[:, 0] = strips_ref[:, 0]
        xpad[:, 1] = strips_ref[:, 0]

    @pl.when(place < last)
    def _():
        up.wait_recv()

    @pl.when(place == last)
    def _():
        xpad[:, rows + 2] = strips_ref[:, 1]
        xpad[:, rows + 3] = strips_ref[:, 1]

    def border(frame, carry):
        hidden_rows(frame, 0)
        hidden_rows(frame, rows)
        return carry

    lax.fori_loop(0, nloc, border, 0)

    @pl.when(place == 0)
    def _():
        hpad[:, 0] = strips_ref[:, 0]

    @pl.when(place == last)
    def _():
        hpad[:, rows + 1] = strips_ref[:, 1]

    def there(h, k):
        row = peer_of(k) * share + h
        return pltpu.make_async_remote_copy(
            sbuf.at[row], rbuf.at[h, pl.ds(me * nloc, nloc)],
            there_send.at[h, k], there_recv.at[h, k],
            device_id={"tm": peer_of(k)}, device_id_type=MESH,
        )

    pending = None
    for h in range(share):
        for k in list(range(2, peers)) + [1, 0]:
            row = peer_of(k) * share + h

            def second_rows(i, carry, row=row, h=h, k=k):
                frames = pl.ds(i * 2, 2)
                taps = [hpad[frames, row + dy].reshape(2 * width, chans) for dy in range(3)]
                second = conv_taps(taps, wcat[1], width)
                resid = xpad[frames, row + 2].astype(jnp.float32) + second.reshape(2, width, chans)
                if k == 0:
                    rbuf[h, pl.ds(me * nloc + i * 2, 2)] = resid.astype(jnp.bfloat16)
                else:
                    sbuf[row, frames] = resid.astype(jnp.bfloat16)
                return carry

            lax.fori_loop(0, nloc // 2, second_rows, 0)
            if pending is not None:
                there(*pending).start()
            pending = (h, k) if k else None

    per_row = width // STEP
    chunks_per_row = per_row // CHUNK
    total = share * per_row

    def chunk_cols(c):
        h = c // chunks_per_row
        start = pl.multiple_of(lax.rem(c, chunks_per_row) * (CHUNK * STEP), CHUNK * STEP)
        return h, pl.ds(start, CHUNK * STEP)

    def back(c, k):
        h, cols = chunk_cols(c)
        return pltpu.make_async_remote_copy(
            abuf.at[h, pl.ds(peer_of(k) * nloc, nloc), cols],
            o_ref.at[:, me * share + h, cols],
            back_send.at[c, k], back_recv.at[c, k],
            device_id={"tm": peer_of(k)}, device_id_type=MESH,
        )

    def keep(c):
        h, cols = chunk_cols(c)
        return pltpu.make_async_copy(
            abuf.at[h, pl.ds(me * nloc, nloc), cols], o_ref.at[:, me * share + h, cols], own_sem.at[c]
        )

    def send_back(c):
        for k in list(range(2, peers)) + [1]:
            back(c, k).start()
        keep(c).start()

    def step(s, carry):
        h = s // per_row
        inner = lax.rem(s, per_row)

        @pl.when(inner == 0)
        def _():
            for k in range(1, peers):
                there(h, k).wait_recv()

        cols = pl.ds(pl.multiple_of(inner * STEP, STEP), STEP)
        x = rbuf[h, :, cols, :].astype(jnp.float32)
        halves = [
            attend_pixels(
                x[:, j * 8 : j * 8 + 8], qkv_ref[...], gain_ref[...], outw_ref[...],
                mask_ref[...], heads_of,
            )
            for j in range(STEP // 8)
        ]
        abuf[h, :, cols, :] = jnp.concatenate(halves, axis=1).astype(jnp.bfloat16)

        @pl.when(lax.rem(s, CHUNK) == CHUNK - 1)
        def _():
            send_back(s // CHUNK)

        return carry

    lax.fori_loop(0, total, step, 0)

    @pl.when(place > 0)
    def _():
        up.wait_send()

    @pl.when(place < last)
    def _():
        down.wait_send()

    for h in range(share):
        for k in range(1, peers):
            there(h, k).wait_send()

    def drain(c, carry):
        for k in range(1, peers):
            back(c, k).wait()
        keep(c).wait()
        return carry

    lax.fori_loop(0, total // CHUNK, drain, 0)


def on_device(frames_in, boundary, conv_first, conv_second, norm_gain, qkv_weight, out_weight):
    nloc, rows, width, chans = frames_in.shape
    peers = lax.axis_size("tm")
    spaces = lax.axis_size("space")
    nframes = nloc * peers
    share = rows // peers
    chunks = share * width // (STEP * CHUNK)
    times = lax.axis_index("tm") * nloc + jnp.arange(nloc, dtype=jnp.int32)
    weights = interp_matrix(times)
    strips = jnp.einsum("tk,kscx->tscx", weights, boundary.astype(jnp.float32)).astype(jnp.bfloat16)
    vmem = pl.BlockSpec(memory_space=pltpu.VMEM)
    hbm = pl.BlockSpec(memory_space=pl.ANY)
    bf16 = jnp.bfloat16
    dma = pltpu.SemaphoreType.DMA
    return pl.pallas_call(
        functools.partial(block_kernel, peers, spaces),
        out_shape=jax.ShapeDtypeStruct(frames_in.shape, frames_in.dtype),
        in_specs=[hbm] + [vmem] * 6,
        out_specs=hbm,
        scratch_shapes=[
            pltpu.VMEM((nloc, rows + 4, width, chans), bf16),
            pltpu.VMEM((nloc, rows + 2, width, chans), bf16),
            pltpu.VMEM((rows, nloc, width, chans), bf16),
            pltpu.VMEM((share, nframes, width, chans), bf16),
            pltpu.VMEM((share, nframes, width, chans), bf16),
            pltpu.VMEM((2, 3 * chans, 3 * chans), bf16),
            pltpu.VMEM((nframes * 8, nframes * 8), jnp.float32),
            dma, dma((2,)), dma((2,)), dma((share, peers)), dma((share, peers)),
            dma((chunks, peers)), dma((chunks, peers)), dma((chunks,)),
        ],
        compiler_params=pltpu.CompilerParams(
            collective_id=0, has_side_effects=True, vmem_limit_bytes=48 * 1024 * 1024
        ),
        name="denoise",
    )(frames_in, strips, conv_first, conv_second, norm_gain.reshape(1, chans), qkv_weight, out_weight)


def solution(mesh):
    placed = (P("tm", "space", None, None), P(), P(), P(), P(), P(), P())
    return jax.shard_map(
        on_device,
        mesh=mesh,
        in_specs=placed,
        out_specs=P("tm", "space", None, None),
        check_vma=False,
    )
```

```python
import functools

import jax
import jax.numpy as jnp
from jax import lax
from jax.experimental import pallas as pl
from jax.experimental.pallas import tpu as pltpu
from jax.sharding import PartitionSpec as P

HEADS = 8
FRAMES = 24
COARSE = 5


def interp_matrix(times):
    scaled = times * (COARSE - 1)
    lower = scaled // (FRAMES - 1)
    upper = jnp.minimum(lower + 1, COARSE - 1)
    frac = (scaled - lower * (FRAMES - 1)).astype(jnp.float32) / float(FRAMES - 1)
    levels = jnp.arange(COARSE, dtype=jnp.int32)
    low_hot = (levels[None, :] == lower[:, None]).astype(jnp.float32)
    up_hot = (levels[None, :] == upper[:, None]).astype(jnp.float32)
    return (1.0 - frac)[:, None] * low_hot + frac[:, None] * up_hot


def attend_block(x, qkv_weight, norm_gain, out_weight, mask, heads_of):
    nframes, cells, chans = x.shape
    rows = nframes * 8
    head_dim = chans // HEADS
    parts = [x[:, j : j + 8].reshape(rows, chans) for j in range(0, cells, 8)]
    x = jnp.concatenate(parts, axis=0)
    mean_sq = jnp.mean(x * x, axis=-1, keepdims=True)
    normed = (x * lax.rsqrt(mean_sq + 1e-06) * norm_gain).astype(jnp.bfloat16)
    qkv = jnp.dot(normed, qkv_weight, preferred_element_type=jnp.float32).astype(jnp.bfloat16)
    outs = []
    for g in range(len(parts)):
        mine = qkv[g * rows : (g + 1) * rows]
        query = mine[:, :chans] * jnp.bfloat16(1.0 / head_dim**0.5)
        key_part = mine[:, chans : 2 * chans]
        value = mine[:, 2 * chans :]
        with_ones = jnp.concatenate([value, jnp.ones_like(value)], axis=1)
        picked = jnp.concatenate(
            [jnp.where(heads_of == h, query, jnp.zeros_like(query)) for h in range(HEADS)], axis=0
        )
        scores = lax.dot_general(
            picked, key_part, (((1,), (1,)), ((), ())), preferred_element_type=jnp.float32
        )
        scores = (scores.reshape(HEADS, rows, rows) + mask).reshape(HEADS * rows, rows)
        top = jnp.max(scores, axis=-1, keepdims=True)
        expd = jnp.exp((scores - top).astype(jnp.bfloat16))
        both = jnp.dot(expd, with_ones, preferred_element_type=jnp.float32)
        num, den = both[:rows, :chans], both[:rows, chans:]
        for h in range(1, HEADS):
            piece = both[h * rows : (h + 1) * rows]
            own = heads_of == h
            num = jnp.where(own, piece[:, :chans], num)
            den = jnp.where(own, piece[:, chans:], den)
        outs.append((num / den).astype(jnp.bfloat16))
    attended = jnp.concatenate(outs, axis=0)
    out = x + jnp.dot(attended, out_weight, preferred_element_type=jnp.float32)
    return jnp.concatenate([out[g * rows : (g + 1) * rows].reshape(nframes, 8, chans) for g in range(len(parts))], axis=1)


MESH = pl.DeviceIdType.MESH
STEP = 64
CHUNK = 1


def conv_taps(taps, weight, width):
    cells = jnp.concatenate(taps, axis=1)
    rows = cells.shape[0]
    chans = weight.shape[1] // 3
    wide = jnp.dot(cells, weight, preferred_element_type=jnp.float32)
    col = lax.rem(lax.broadcasted_iota(jnp.int32, (rows, chans), 0), width)
    left = jnp.where(col == 0, 0.0, pltpu.roll(wide[:, :chans], 1, 0))
    right = jnp.where(col == width - 1, 0.0, pltpu.roll(wide[:, 2 * chans :], rows - 1, 0))
    return wide[:, chans : 2 * chans] + left + right


def block_kernel(
    peers, spaces,
    x_ref, strips_ref, w1_ref, w2_ref, gain_ref, qkv_ref, outw_ref, o_ref,
    xpad, hpad, sbuf, rbuf, abuf, wcat, mask_ref,
    local_sem, halo_send, halo_recv, there_send, there_recv, back_send, back_recv, own_sem,
):
    nloc, rows, width, chans = x_ref.shape
    nframes = nloc * peers
    share = rows // peers
    me = lax.axis_index("tm")
    place = lax.axis_index("space")
    last = spaces - 1

    def peer_of(k):
        chip = lax.rem(me // 2 + k // 2, peers // 2)
        return chip * 2 + lax.rem(me + k % 2, 2)

    own_rows = pltpu.make_async_copy(x_ref, xpad.at[:, pl.ds(2, rows)], local_sem)
    own_rows.start()

    barrier = pltpu.get_barrier_semaphore()
    for k in range(1, peers):
        pl.semaphore_signal(barrier, inc=1, device_id={"tm": peer_of(k)}, device_id_type=MESH)

    @pl.when(place > 0)
    def _():
        pl.semaphore_signal(barrier, inc=1, device_id={"space": place - 1}, device_id_type=MESH)

    @pl.when(place < last)
    def _():
        pl.semaphore_signal(barrier, inc=1, device_id={"space": place + 1}, device_id_type=MESH)

    beside = jnp.where(place > 0, 1, 0) + jnp.where(place < last, 1, 0)
    pl.semaphore_wait(barrier, peers - 1 + beside)

    up = pltpu.make_async_remote_copy(
        x_ref.at[:, pl.ds(0, 2)], xpad.at[:, pl.ds(rows + 2, 2)],
        halo_send.at[0], halo_recv.at[0], device_id={"space": place - 1}, device_id_type=MESH,
    )
    down = pltpu.make_async_remote_copy(
        x_ref.at[:, pl.ds(rows - 2, 2)], xpad.at[:, pl.ds(0, 2)],
        halo_send.at[1], halo_recv.at[1], device_id={"space": place + 1}, device_id_type=MESH,
    )

    @pl.when(place > 0)
    def _():
        up.start()

    @pl.when(place < last)
    def _():
        down.start()

    for which, ref in enumerate((w1_ref, w2_ref)):
        for dy in range(3):
            for dx in range(3):
                wcat[which, dy * chans : (dy + 1) * chans, dx * chans : (dx + 1) * chans] = ref[dy, dx]
    group = nframes * 8
    row_id = lax.broadcasted_iota(jnp.int32, (group, group), 0)
    col_id = lax.broadcasted_iota(jnp.int32, (group, group), 1)
    mask_ref[...] = jnp.where(lax.rem(row_id, 8) == lax.rem(col_id, 8), 0.0, -1e30)
    heads_of = lax.broadcasted_iota(jnp.int32, (group, chans), 1) // (chans // HEADS)

    def hidden_rows(frame, row):
        taps = [xpad[frame, row + dy : row + dy + 2].reshape(2 * width, chans) for dy in range(3)]
        first = conv_taps(taps, wcat[0], width)
        act = (first / (1.0 + jnp.exp(-first))).astype(jnp.bfloat16)
        hpad[frame, row : row + 2] = act.reshape(2, width, chans)

    own_rows.wait()

    def interior(frame, carry):
        for row in range(2, rows, 2):
            hidden_rows(frame, row)
        return carry

    lax.fori_loop(0, nloc, interior, 0)

    @pl.when(place > 0)
    def _():
        down.wait_recv()

    @pl.when(place == 0)
    def _():
        xpad[:, 0] = strips_ref[:, 0]
        xpad[:, 1] = strips_ref[:, 0]

    @pl.when(place < last)
    def _():
        up.wait_recv()

    @pl.when(place == last)
    def _():
        xpad[:, rows + 2] = strips_ref[:, 1]
        xpad[:, rows + 3] = strips_ref[:, 1]

    def border(frame, carry):
        hidden_rows(frame, 0)
        hidden_rows(frame, rows)
        return carry

    lax.fori_loop(0, nloc, border, 0)

    @pl.when(place == 0)
    def _():
        hpad[:, 0] = strips_ref[:, 0]

    @pl.when(place == last)
    def _():
        hpad[:, rows + 1] = strips_ref[:, 1]

    def there(h, k):
        row = peer_of(k) * share + h
        return pltpu.make_async_remote_copy(
            sbuf.at[row], rbuf.at[h, pl.ds(me * nloc, nloc)],
            there_send.at[h, k], there_recv.at[h, k],
            device_id={"tm": peer_of(k)}, device_id_type=MESH,
        )

    pending = None
    for h in range(share):
        for k in list(range(2, peers)) + [1, 0]:
            row = peer_of(k) * share + h

            taps = [hpad[:, row + dy].reshape(nloc * width, chans) for dy in range(3)]
            second = conv_taps(taps, wcat[1], width).reshape(nloc, width, chans)
            resid = (xpad[:, row + 2].astype(jnp.float32) + second).astype(jnp.bfloat16)
            if k == 0:
                rbuf[h, pl.ds(me * nloc, nloc)] = resid
            else:
                sbuf[row] = resid
            if pending is not None:
                there(*pending).start()
            pending = (h, k) if k else None

    per_row = width // STEP
    chunks_per_row = per_row // CHUNK
    total = share * per_row

    def chunk_cols(c):
        h = c // chunks_per_row
        start = pl.multiple_of(lax.rem(c, chunks_per_row) * (CHUNK * STEP), CHUNK * STEP)
        return h, pl.ds(start, CHUNK * STEP)

    def back(c, k):
        h, cols = chunk_cols(c)
        return pltpu.make_async_remote_copy(
            abuf.at[h, pl.ds(peer_of(k) * nloc, nloc), cols],
            o_ref.at[:, me * share + h, cols],
            back_send.at[c, k], back_recv.at[c, k],
            device_id={"tm": peer_of(k)}, device_id_type=MESH,
        )

    def keep(c):
        h, cols = chunk_cols(c)
        return pltpu.make_async_copy(
            abuf.at[h, pl.ds(me * nloc, nloc), cols], o_ref.at[:, me * share + h, cols], own_sem.at[c]
        )

    def send_back(c):
        for k in list(range(2, peers)) + [1]:
            back(c, k).start()
        keep(c).start()

    def step(s, carry):
        h = s // per_row
        inner = lax.rem(s, per_row)

        @pl.when(inner == 0)
        def _():
            for k in range(1, peers):
                there(h, k).wait_recv()

        cols = pl.ds(pl.multiple_of(inner * STEP, STEP), STEP)
        x = rbuf[h, :, cols, :].astype(jnp.float32)
        mixed = attend_block(
            x, qkv_ref[...], gain_ref[...], outw_ref[...], mask_ref[...], heads_of
        )
        abuf[h, :, cols, :] = mixed.astype(jnp.bfloat16)

        @pl.when(lax.rem(s, CHUNK) == CHUNK - 1)
        def _():
            send_back(s // CHUNK)

        return carry

    lax.fori_loop(0, total, step, 0)

    @pl.when(place > 0)
    def _():
        up.wait_send()

    @pl.when(place < last)
    def _():
        down.wait_send()

    for h in range(share):
        for k in range(1, peers):
            there(h, k).wait_send()

    def drain(c, carry):
        for k in range(1, peers):
            back(c, k).wait()
        keep(c).wait()
        return carry

    lax.fori_loop(0, total // CHUNK, drain, 0)


def on_device(frames_in, boundary, conv_first, conv_second, norm_gain, qkv_weight, out_weight):
    nloc, rows, width, chans = frames_in.shape
    peers = lax.axis_size("tm")
    spaces = lax.axis_size("space")
    nframes = nloc * peers
    share = rows // peers
    chunks = share * width // (STEP * CHUNK)
    times = lax.axis_index("tm") * nloc + jnp.arange(nloc, dtype=jnp.int32)
    weights = interp_matrix(times)
    strips = jnp.einsum("tk,kscx->tscx", weights, boundary.astype(jnp.float32)).astype(jnp.bfloat16)
    vmem = pl.BlockSpec(memory_space=pltpu.VMEM)
    hbm = pl.BlockSpec(memory_space=pl.ANY)
    bf16 = jnp.bfloat16
    dma = pltpu.SemaphoreType.DMA
    return pl.pallas_call(
        functools.partial(block_kernel, peers, spaces),
        out_shape=jax.ShapeDtypeStruct(frames_in.shape, frames_in.dtype),
        in_specs=[hbm] + [vmem] * 6,
        out_specs=hbm,
        scratch_shapes=[
            pltpu.VMEM((nloc, rows + 4, width, chans), bf16),
            pltpu.VMEM((nloc, rows + 2, width, chans), bf16),
            pltpu.VMEM((rows, nloc, width, chans), bf16),
            pltpu.VMEM((share, nframes, width, chans), bf16),
            pltpu.VMEM((share, nframes, width, chans), bf16),
            pltpu.VMEM((2, 3 * chans, 3 * chans), bf16),
            pltpu.VMEM((nframes * 8, nframes * 8), jnp.float32),
            dma, dma((2,)), dma((2,)), dma((share, peers)), dma((share, peers)),
            dma((chunks, peers)), dma((chunks, peers)), dma((chunks,)),
        ],
        compiler_params=pltpu.CompilerParams(
            collective_id=0, has_side_effects=True, vmem_limit_bytes=48 * 1024 * 1024
        ),
        name="denoise",
    )(frames_in, strips, conv_first, conv_second, norm_gain.reshape(1, chans), qkv_weight, out_weight)


def solution(mesh):
    placed = (P("tm", "space", None, None), P(), P(), P(), P(), P(), P())
    return jax.shard_map(
        on_device,
        mesh=mesh,
        in_specs=placed,
        out_specs=P("tm", "space", None, None),
        check_vma=False,
    )
```
